256 devices in a mesh: section: 8 (over z), dp: 32 (over y, x, core).
Axes of the slice: x: 4, y: 4, z: 8, core: 2. Of those that a mesh axis runs over, the one named last changes fastest.
Arguments:
- held: bfloat16 [8, 2, 4096, 2048], P('section', None, 'dp'), may hold values from -70 to 70
- norm_gain: float32 [8, 2048], P('section'), may hold values from 0.3 to 3
- w_qkv: bfloat16 [8, 2048, 2560], P('section', None, 'dp'), may hold values from -1 to 1
- q_gain: float32 [8, 128], P('section'), may hold values from 0.5 to 7
- k_gain: float32 [8, 128], P('section'), may hold values from 0.5 to 7
- w_out: bfloat16 [8, 2048, 2048], P('section', None, 'dp'), may hold values from -0.125 to 0.125
- lengths: int32 [8, 2, 8], P('section'), may hold values from 1 to 2048, 4096 in all within a row
Outputs:
- handed: bfloat16 [8, 2, 4096, 2048], P('section', None, 'dp')
The draws below stay inside these ranges and needn't reach their ends.
Inputs may be any that keep to these rules, and one draw needn't show every extreme that they name: Each row lists the 8 document lengths of one packed micro-batch in order; they sum to 4096 and the longest is exactly 2048.
All inputs are finite; a program needn't handle non-finite values.
Results may differ from the reference program's by a relative error of at most 0.0086.
Values may be sent and summed in bfloat16 or wider, within the bound.
A program may use at most 128 MiB of HBM per device.

```python
import math
import jax
import jax.numpy as jnp
import numpy as np
from jax import lax

D = 2048
HEADS = 16
KV_HEADS = 2
HEAD = 128
MICRO = 2
DOCS = 8
GROUP = 8
INNER = 2048
QKV = 2560
TOKENS = 4096
DOC_MOST = 2048
N_SECTION = 8


def draw_held(key, part):
    first = jax.random.fold_in(key, 0)
    shape = (N_SECTION, MICRO, TOKENS, D)
    base = jax.random.truncated_normal(first, -6.0, 6.0, shape, jnp.float32)
    return base.astype(jnp.bfloat16)


def draw_w_qkv(key, part):
    first = jax.random.fold_in(key, 0)
    weights = jax.random.truncated_normal(first, -4.0, 4.0, (N_SECTION, D, QKV), jnp.float32) * D ** (-0.5)
    return weights.astype(jnp.bfloat16)


def gain_draw(key, salt):
    salted = jax.random.fold_in(key, salt)
    return jnp.exp(jax.random.uniform(salted, (N_SECTION, HEAD), jnp.float32, math.log(0.5), math.log(2.0)))


def draw_q_gain(key, part):
    return gain_draw(key, 11)


def draw_k_gain(key, part):
    return gain_draw(key, 12)


def levels(key, extent, cuts, smallest, top_value):
    factor_of = 1.0
    for dim, blocks in cuts:
        draws = jax.random.uniform(jax.random.fold_in(jax.random.fold_in(key, 6), dim), (blocks,), jnp.float32, smallest / len(cuts), top_value / len(cuts))
        factor_of = factor_of * jnp.repeat(jnp.exp(draws), extent[dim] // blocks).reshape((-1,) + (1,) * (len(extent) - 1 - dim))
    return factor_of


def profile(amount, total, limit, skew):
    portions = [(1 << 20) // math.isqrt(rank ** skew) + 1 for rank in range(2, amount + 1)]
    rest, holding = total - limit - (amount - 1), [1] * (amount - 1)
    while rest > 0:
        candidates = [i for i in range(amount - 1) if holding[i] < limit]
        pool, budget = sum([portions[i] for i in candidates]), rest
        for i in candidates:
            more = min(limit - holding[i], max(1, budget * portions[i] // pool), rest)
            holding[i] = holding[i] + more
            rest = rest - more
    return np.array([limit] + holding)


def uneven(rng, number_of, total, limit, slope):
    if number_of == 2:
        one = jax.random.randint(rng, (), max(1, total - limit), min(limit, total - 1) + 1)
        return jnp.stack([one, total - one])
    sizes = jnp.asarray(profile(number_of, total, limit, slope), jnp.int32)
    twos = (number_of - 1) // 2
    source_of, sink = sizes[1:1 + 2 * twos:2], sizes[2:2 + 2 * twos:2]
    room = jnp.minimum(source_of - 1, limit - sink)
    passed = jax.random.randint(jax.random.fold_in(rng, 1), (twos,), 0, 1 << 20) % (room + 1)
    sizes = sizes.at[1:1 + 2 * twos:2].set(source_of - passed).at[2:2 + 2 * twos:2].set(sink + passed)
    return sizes[jax.random.permutation(jax.random.fold_in(rng, 2), number_of)]


def normal_values(own_key, extent, scale, most, cuts=(), kind=jnp.bfloat16):
    entries = jax.random.normal(own_key, extent, jnp.float32) * scale
    if len(cuts) > 0:
        entries = levels(own_key, extent, cuts, -0.22, 0.18) * entries
    return jnp.clip(entries, min=-most, max=most).astype(kind)


def setup_inputs(seed: int = 0) -> dict:
    key_of = jax.random.split(jax.random.key(seed), 8)
    return {
        "held": draw_held(jax.random.fold_in(key_of[7], 71), 0),
        "norm_gain": jnp.clip(jnp.exp(math.log(3.0) - 2.3025851 * jax.random.uniform(key_of[1], (N_SECTION, D), jnp.float32) ** levels(key_of[1], (N_SECTION, D), ((0, 8),), -0.2, 0.2)), 0.3, 3.0),
        "w_qkv": draw_w_qkv(jax.random.fold_in(key_of[7], 71), 0),
        "q_gain": draw_q_gain(jax.random.fold_in(key_of[7], 71), 0),
        "k_gain": draw_k_gain(jax.random.fold_in(key_of[7], 71), 0),
        "w_out": normal_values(key_of[5], (N_SECTION, INNER, D), INNER ** -0.5, 0.125, ((0, 8), (2, 32))),
        "lengths": jax.vmap(lambda own: uneven(own, DOCS, TOKENS, DOC_MOST, 2))(jax.random.split(key_of[6], N_SECTION * MICRO)).reshape((N_SECTION, MICRO, DOCS)).astype(jnp.int32),
    }


EPSILON = 1e-06
THETA = 1000000.0

def rms_scale(values, gain):
    return values * lax.rsqrt(lax.optimization_barrier(jnp.mean(values * values, axis=-1, keepdims=True)) + EPSILON) * gain

def rotary(values, places):
    width = values.shape[-1]
    middle = width // 2
    spacing = jnp.exp(jnp.arange(middle, dtype=jnp.float32) * (-2.0 * math.log(THETA) / width))
    angle = places.astype(jnp.float32)[..., None] * spacing
    cosine = jnp.cos(angle)[..., None, :]
    sine = jnp.sin(angle)[..., None, :]
    former = values[..., :middle]
    latter = values[..., middle:]
    return jnp.concatenate([former * cosine - latter * sine, latter * cosine + former * sine], axis=-1)

def layer(resident_bf, gain, weight_in, query_gain, key_gain, weight_out, doc_lengths):
    total = resident_bf.shape[0]
    inner = HEADS * HEAD
    key_width = KV_HEADS * HEAD
    resident = resident_bf.astype(jnp.float32)
    normed = rms_scale(resident, gain).astype(jnp.bfloat16)
    projected = jnp.dot(normed, weight_in, preferred_element_type=jnp.float32)
    index = jnp.arange(total, dtype=jnp.int32)
    ends = jnp.cumsum(doc_lengths)
    before = (ends[None, :] <= index[:, None]).astype(jnp.int32)
    doc_start = lax.optimization_barrier(jnp.sum(before * doc_lengths[None, :], axis=-1))
    doc_number = lax.optimization_barrier(jnp.sum(before, axis=-1))
    places = index - doc_start
    queries = rotary(rms_scale(projected[:, :inner].reshape(total, HEADS, HEAD), query_gain), places).astype(jnp.bfloat16)
    keys = rotary(rms_scale(projected[:, inner:inner + key_width].reshape(total, KV_HEADS, HEAD), key_gain), places).astype(jnp.bfloat16)
    values = projected[:, inner + key_width:].reshape(total, KV_HEADS, HEAD).astype(jnp.bfloat16)
    block = math.gcd(total, 512)
    reach = min(total, block + DOC_MOST)

    def attend(number):
        first = (number * block).astype(jnp.int32)
        key_first = jnp.clip(first + block - reach, 0, total - reach).astype(jnp.int32)
        query_rows = lax.dynamic_slice_in_dim(queries, first, block, 0).reshape(block, KV_HEADS, GROUP, HEAD).astype(jnp.float32)
        key_rows = lax.dynamic_slice_in_dim(keys, key_first, reach, 0).astype(jnp.float32)
        value_rows = lax.dynamic_slice_in_dim(values, key_first, reach, 0).astype(jnp.float32)
        query_index = first + jnp.arange(block, dtype=jnp.int32)
        key_index = key_first + jnp.arange(reach, dtype=jnp.int32)
        query_doc = lax.dynamic_slice_in_dim(doc_number, first, block, 0)
        key_doc = lax.dynamic_slice_in_dim(doc_number, key_first, reach, 0)
        scores = jnp.einsum('qkgd,nkd->kgqn', query_rows, key_rows) / math.sqrt(HEAD)
        allowed = (query_doc[:, None] == key_doc[None, :]) & (query_index[:, None] >= key_index[None, :])
        highest = lax.optimization_barrier(jnp.max(jnp.where(allowed, scores, -jnp.inf), axis=-1, keepdims=True))
        weights = lax.optimization_barrier(jnp.where(allowed, jnp.exp(scores - highest), 0.0).astype(jnp.bfloat16)).astype(jnp.float32)
        numer = jnp.einsum('kgqn,nkd->qkgd', weights, value_rows)
        denom = jnp.transpose(lax.optimization_barrier(jnp.sum(weights, axis=-1)), (2, 0, 1))
        return (numer / denom[..., None]).astype(jnp.bfloat16).reshape(block, inner)
    attended = lax.map(attend, jnp.arange(total // block, dtype=jnp.int32)).reshape(total, inner)
    mixed = jnp.dot(attended, weight_out, preferred_element_type=jnp.float32)
    return (resident + mixed).astype(jnp.bfloat16)

def reference(held, norm_gain, w_qkv, q_gain, k_gain, w_out, lengths):
    sections = held.shape[0]
    micro = held.shape[1]

    def one(number):
        section = number // micro
        which = number % micro
        return layer(held[section, which], norm_gain[section], w_qkv[section], q_gain[section], k_gain[section], w_out[section], lengths[section, which])
    results = lax.map(one, jnp.arange(sections * micro, dtype=jnp.int32)).reshape(held.shape)
    return jnp.roll(results, 1, axis=0)
```

```python
import functools
import math

import jax
import jax.numpy as jnp
from jax import lax
from jax.experimental import pallas as pl
from jax.experimental.pallas import tpu as pltpu
from jax.sharding import PartitionSpec as P

N_RECV = 40
N_SIB = 32

class Gather:
    def __init__(self, piece, send_sems, recv_sems, sib_send, sib_recv, own_src=None, order=("A","B")):
        self.piece = piece
        self.ss, self.rs, self.bs, self.br = send_sems, recv_sems, sib_send, sib_recv
        me = lax.axis_index("dp")
        self.me = me
        self.c = lax.rem(me, 2)
        chip = me // 2
        self.x = lax.rem(chip, 4)
        self.y = chip // 4
        self.order = order
        self.sends = []
        self.sib_n = 0
        self.sibs = []

    def dev(self, ox, oy):
        return (lax.rem(self.y + 4 + oy, 4) * 4 + lax.rem(self.x + 4 + ox, 4)) * 2 + self.c

    def off(self, tree, first, second):
        return (first, second) if tree == "A" else (second, first)

    def role(self, tree, kind, d, k=0):
        base = 0 if tree == "A" else 20
        di = 0 if d > 0 else 1
        return base + {"1": 0, "1q": 2, "2": 4, "2q": 12}[kind] + di + 2 * k

    def copy(self, slot, tree, quarter, role, target):
        ref = self.piece(slot, tree, quarter)
        cp = pltpu.make_async_remote_copy(ref, ref, self.ss.at[role], self.rs.at[role],
            device_id={"dp": target}, device_id_type=pl.DeviceIdType.MESH)
        return cp

    def send(self, slot, tree, quarter, kind, d, k, target):
        cp = self.copy(slot, tree, quarter, self.role(tree, kind, d, k), target)
        cp.start()
        self.sends.append(cp)

    def wait(self, slot, tree, quarter, kind, d, k=0):
        self.copy(slot, tree, quarter, self.role(tree, kind, d, k), self.me).wait_recv()

    def sib_copy(self, slot, tree, n):
        ref = self.piece(slot, tree, None)
        return pltpu.make_async_remote_copy(ref, ref, self.bs.at[n], self.br.at[n],
            device_id={"dp": self.me + 1 - 2 * self.c}, device_id_type=pl.DeviceIdType.MESH)

    def to_sibling(self, slot, other, tree):
        n = self.sib_n
        self.sib_n += 1
        cp = self.sib_copy(slot, tree, n)
        cp.start()
        self.sibs.append((cp, self.sib_copy(other, tree, n)))

    FIRST = (0, -1, 1, 2)

    def slot(self, tree, first, second):
        return self.dev(*self.off(tree, first, second))

    def fan(self, tree, k, part=None):
        s = self.slot(tree, self.FIRST[k], 0)
        for d in (1, -1):
            self.send(s, tree, None, "2", d, k, self.slot(tree, 0, d))
        self.sib(s, tree)

    def sib(self, s, tree):
        if self.bs is not None:
            self.to_sibling(s, s + 1 - 2 * self.c, tree)

    def steps(self):
        out = []
        def s0():
            for t in self.order:
                for d in (1, -1):
                    self.send(self.me, t, None, "1", d, 0, self.slot(t, d, 0))
            for t in self.order:
                self.fan(t, 0)
        out.append(s0)
        def s1():
            for d in (1, -1):
                for t in self.order:
                    s = self.slot(t, -d, 0)
                    self.wait(s, t, None, "1", d)
                    self.send(s, t, 0 if d > 0 else 1, "1q", d, 0, self.slot(t, d, 0))
            for t in self.order:
                for k in (1, 2):
                    self.fan(t, k)
        out.append(s1)
        def s2():
            for t in self.order:
                s = self.slot(t, 2, 0)
                self.wait(s, t, 0, "1q", 1)
                self.wait(s, t, 1, "1q", -1)
                self.fan(t, 3)
        out.append(s2)
        def s3(k):
            def f():
                for d in (1, -1):
                    for t in self.order:
                        s = self.slot(t, self.FIRST[k], -d)
                        self.wait(s, t, None, "2", d, k)
                        self.send(s, t, 0 if d > 0 else 1, "2q", d, k, self.slot(t, 0, d))
                        self.sib(s, t)
            return f
        def s4(k):
            def f():
                for t in self.order:
                    s = self.slot(t, self.FIRST[k], 2)
                    self.wait(s, t, 0, "2q", 1, k)
                    self.wait(s, t, 1, "2q", -1, k)
                    self.sib(s, t)
            return f
        out.insert(2, s3(0))
        out += [s3(1), s4(0), s3(2), s4(1), s3(3), s4(2), s4(3)]
        return out

    def wait_siblings(self):
        for _, r in self.sibs:
            r.wait_recv()

    def finish(self):
        for cp in self.sends:
            cp.wait_send()
        for cp, _ in self.sibs:
            cp.wait_send()

def neighbours():
    me = lax.axis_index("dp")
    c = lax.rem(me, 2); chip = me // 2; x = lax.rem(chip, 4); y = chip // 4
    def dev(ox, oy):
        return (lax.rem(y + 4 + oy, 4) * 4 + lax.rem(x + 4 + ox, 4)) * 2 + c
    return [dev(1,0), dev(-1,0), dev(0,1), dev(0,-1), me + 1 - 2*c]

def entry_barrier():
    b = pltpu.get_barrier_semaphore()
    ns = neighbours()
    for n in ns:
        pl.semaphore_signal(b, inc=1, device_id={"dp": n}, device_id_type=pl.DeviceIdType.MESH)
    pl.semaphore_wait(b, len(ns))


def gather_kernel(split_rows, w_ref, o_ref, ss, rs, bs, br, ls):
    entry_barrier()
    me = lax.axis_index("dp")
    own = pltpu.make_async_copy(w_ref, o_ref.at[me], ls)
    own.start()
    own.wait()

    def piece(slot, tree, quarter):
        if split_rows:
            half = w_ref.shape[0] // 2
            base = 0 if tree == "A" else half
            if quarter is None:
                return o_ref.at[slot, pl.ds(base, half), :]
            return o_ref.at[slot, pl.ds(base + half // 2 * quarter, half // 2), :]
        half = w_ref.shape[1] // 2
        base = 0 if tree == "A" else half
        if quarter is None:
            return o_ref.at[slot, :, pl.ds(base, half)]
        return o_ref.at[slot, :, pl.ds(base + half // 2 * quarter, half // 2)]

    gather = Gather(piece, ss, rs, bs, br)
    for step in gather.steps():
        step()
    gather.wait_siblings()
    gather.finish()


def gather_all(shard, number, split_rows=False):
    return pl.pallas_call(
        functools.partial(gather_kernel, split_rows),
        out_shape=jax.ShapeDtypeStruct((32,) + shard.shape, jnp.bfloat16),
        in_specs=[pl.BlockSpec(memory_space=pl.ANY)],
        out_specs=pl.BlockSpec(memory_space=pl.ANY),
        scratch_shapes=[
            pltpu.SemaphoreType.DMA((40,)),
            pltpu.SemaphoreType.DMA((40,)),
            pltpu.SemaphoreType.DMA((32,)),
            pltpu.SemaphoreType.DMA((32,)),
            pltpu.SemaphoreType.DMA,
        ],
        compiler_params=pltpu.CompilerParams(collective_id=number, has_side_effects=True),
        name=f"gather_{number}",
    )(shard)


HEADS = 16
KV_HEADS = 2
HEAD = 128
GROUP = 8


EPSILON = 1e-06
THETA = 1000000.0
NEGATIVE = -1e30


def from_behind(value, axis, steps):
    count = lax.axis_size(axis)
    pairs = [(source, (source + steps) % count) for source in range(count)]
    return lax.ppermute(value, axis, pairs)


def rms_scale(values, gain):
    return values * lax.rsqrt(jnp.mean(values * values, axis=-1, keepdims=True) + EPSILON) * gain


def rotary(values, places):
    width = values.shape[-1]
    middle = width // 2
    spacing = jnp.exp(jnp.arange(middle, dtype=jnp.float32) * (-2.0 * math.log(THETA) / width))
    angle = places.astype(jnp.float32)[..., None] * spacing
    cosine = jnp.cos(angle)[..., None, :]
    sine = jnp.sin(angle)[..., None, :]
    former = values[..., :middle]
    latter = values[..., middle:]
    return jnp.concatenate(
        [former * cosine - latter * sine, latter * cosine + former * sine], axis=-1
    )


def locate(positions, doc_lengths):
    count = doc_lengths.shape[-1]
    upto = jnp.arange(count)[None, :] <= jnp.arange(count)[:, None]
    ends = jnp.sum(jnp.where(upto[None], doc_lengths[:, None, :], 0), axis=-1)
    before = (ends[:, None, :] <= positions[None, :, None]).astype(jnp.int32)
    return (jnp.sum(before, axis=-1), jnp.sum(before * doc_lengths[:, None, :], axis=-1))


def attend_rows(query_rows, key_rows, value_rows, allowed):
    scores = jnp.einsum(
        "kqd,nkd->kqn", query_rows, key_rows, preferred_element_type=jnp.float32
    ) / math.sqrt(HEAD)
    highest = jnp.max(jnp.where(allowed[None], scores, NEGATIVE), axis=-1)
    weights = jnp.where(allowed[None], jnp.exp(scores - highest[..., None]), 0.0).astype(
        jnp.bfloat16
    )
    total = jnp.sum(weights.astype(jnp.float32), axis=-1)
    summed = jnp.einsum("kqn,nkd->kqd", weights, value_rows, preferred_element_type=jnp.float32)
    return summed / total[..., None]


def on_device(held, norm_gain, w_qkv, q_gain, k_gain, w_out, lengths):
    micro = held.shape[1]
    rows = held.shape[2]
    width = held.shape[3]
    inner = HEADS * HEAD
    key_width = KV_HEADS * HEAD
    middle = rows // 2
    devices = lax.axis_size("dp")
    here = lax.axis_index("dp")
    total_tokens = rows * devices
    doc_most = min(4096, total_tokens // 2)
    reach = min(total_tokens, doc_most + middle)
    doc_lengths = lengths[0]
    resident = held[0].astype(jnp.float32).reshape(micro * rows, width)
    normed = rms_scale(resident, norm_gain[0]).astype(jnp.bfloat16)
    w_in = gather_all(w_qkv[0].T, 0).reshape(-1, width)
    projected = lax.dot_general(
        normed, w_in, (((1,), (1,)), ((), ())), preferred_element_type=jnp.float32
    ).reshape(micro, rows, inner + 2 * key_width)
    own_index = here * rows + jnp.arange(rows, dtype=jnp.int32)
    own_start = locate(own_index, doc_lengths)[1]
    places = own_index[None, :] - own_start
    queries = rotary(
        rms_scale(projected[..., :inner].reshape(micro, rows, HEADS, HEAD), q_gain[0]), places
    ).astype(jnp.bfloat16)
    keys = rotary(
        rms_scale(
            projected[..., inner : inner + key_width].reshape(micro, rows, KV_HEADS, HEAD),
            k_gain[0],
        ),
        places,
    ).astype(jnp.bfloat16)
    values = projected[..., inner + key_width :].astype(jnp.bfloat16)
    packed = jnp.concatenate([keys.reshape(micro, rows, key_width), values], axis=-1)
    gathered = gather_all(packed.reshape(micro * rows, -1), 1, True)
    gathered = gathered.reshape(devices, micro, rows, -1).transpose(1, 0, 2, 3)
    gathered = gathered.reshape(micro, total_tokens, -1)
    latter_queries = queries[:, middle:]
    latter_index = own_index[middle:]
    group_index = jnp.stack([own_index[:middle], latter_index])
    group_doc = locate(group_index.reshape(-1), doc_lengths)[0].reshape(micro, 2, middle)
    arranged = jnp.stack([queries[:, :middle], latter_queries], axis=1)
    arranged = arranged.reshape(micro, 2, middle, KV_HEADS, GROUP, HEAD).transpose(0, 1, 3, 4, 2, 5)
    arranged = arranged.reshape(micro, 2, KV_HEADS, GROUP * middle, HEAD)
    row_index = jnp.tile(group_index, (1, GROUP))
    row_doc = jnp.tile(group_doc, (1, 1, GROUP))
    finished = []
    for which_micro in range(micro):
        for which_half in range(2):
            first = group_index[which_half, 0]
            key_first = jnp.clip(first + middle - reach, 0, total_tokens - reach)
            window = lax.dynamic_slice_in_dim(gathered[which_micro], key_first, reach, 0)
            key_index = key_first + jnp.arange(reach, dtype=jnp.int32)
            key_doc = locate(key_index, doc_lengths[which_micro : which_micro + 1])[0][0]
            key_part = window[:, :key_width].reshape(reach, KV_HEADS, HEAD)
            value_part = window[:, key_width:].reshape(reach, KV_HEADS, HEAD)
            allowed = (row_doc[which_micro, which_half][:, None] == key_doc[None, :]) & (
                row_index[which_half][:, None] >= key_index[None, :]
            )
            ratio = attend_rows(
                arranged[which_micro, which_half], key_part, value_part, allowed
            ).astype(jnp.bfloat16)
            finished.append(
                ratio.reshape(KV_HEADS, GROUP, middle, HEAD)
                .transpose(2, 0, 1, 3)
                .reshape(middle, inner)
            )
    former_part = jnp.stack(finished[0::2])
    latter_part = jnp.stack(finished[1::2])
    attended = jnp.concatenate([former_part, latter_part], axis=1).reshape(micro * rows, inner)
    w_last = gather_all(w_out[0].T, 2).reshape(-1, inner)
    mixed = lax.dot_general(
        attended, w_last, (((1,), (1,)), ((), ())), preferred_element_type=jnp.float32
    )
    result = (resident + mixed).astype(jnp.bfloat16).reshape(1, micro, rows, width)
    return from_behind(result, "section", 1)


def solution(mesh):
    in_specs = (
        P("section", None, "dp", None),
        P("section", None),
        P("section", None, "dp"),
        P("section", None),
        P("section", None),
        P("section", None, "dp"),
        P("section", None, None),
    )
    out_specs = P("section", None, "dp", None)
    return jax.shard_map(
        on_device, mesh=mesh, in_specs=in_specs, out_specs=out_specs, check_vma=False
    )
```

```python
import math

import jax
import jax.numpy as jnp
from jax import lax
from jax.experimental import pallas as pl
from jax.experimental.pallas import tpu as pltpu
from jax.sharding import PartitionSpec as P

HEADS = 16
KV_HEADS = 2
HEAD = 128
GROUP = 8
MICRO = 2
ROWS = 128
WIDTH = 2048
SLOTS = 32
WINDOW = 17
EPSILON = 1e-06
THETA = 1000000.0
NEGATIVE = -1e30
MESH = pl.DeviceIdType.MESH


class Gather:
    def __init__(self, piece, send_sems, recv_sems, sib_send, sib_recv, own_src=None, order=("A","B")):
        self.piece = piece
        self.ss, self.rs, self.bs, self.br = send_sems, recv_sems, sib_send, sib_recv
        me = lax.axis_index("dp")
        self.me = me
        self.c = lax.rem(me, 2)
        chip = me // 2
        self.x = lax.rem(chip, 4)
        self.y = chip // 4
        self.order = order
        self.sends = []
        self.sib_n = 0
        self.sibs = []

    def dev(self, ox, oy):
        return (lax.rem(self.y + 4 + oy, 4) * 4 + lax.rem(self.x + 4 + ox, 4)) * 2 + self.c

    def off(self, tree, first, second):
        return (first, second) if tree == "A" else (second, first)

    def role(self, tree, kind, d, k=0):
        base = 0 if tree == "A" else 20
        di = 0 if d > 0 else 1
        return base + {"1": 0, "1q": 2, "2": 4, "2q": 12}[kind] + di + 2 * k

    def copy(self, slot, tree, quarter, role, target):
        ref = self.piece(slot, tree, quarter)
        cp = pltpu.make_async_remote_copy(ref, ref, self.ss.at[role], self.rs.at[role],
            device_id={"dp": target}, device_id_type=pl.DeviceIdType.MESH)
        return cp

    def send(self, slot, tree, quarter, kind, d, k, target):
        cp = self.copy(slot, tree, quarter, self.role(tree, kind, d, k), target)
        cp.start()
        self.sends.append(cp)

    def wait(self, slot, tree, quarter, kind, d, k=0):
        self.copy(slot, tree, quarter, self.role(tree, kind, d, k), self.me).wait_recv()

    def sib_copy(self, slot, tree, n):
        ref = self.piece(slot, tree, None)
        return pltpu.make_async_remote_copy(ref, ref, self.bs.at[n], self.br.at[n],
            device_id={"dp": self.me + 1 - 2 * self.c}, device_id_type=pl.DeviceIdType.MESH)

    def to_sibling(self, slot, other, tree):
        n = self.sib_n
        self.sib_n += 1
        cp = self.sib_copy(slot, tree, n)
        cp.start()
        self.sibs.append((cp, self.sib_copy(other, tree, n)))

    FIRST = (0, -1, 1, 2)

    def slot(self, tree, first, second):
        return self.dev(*self.off(tree, first, second))

    def fan(self, tree, k, part=None):
        s = self.slot(tree, self.FIRST[k], 0)
        for d in (1, -1):
            self.send(s, tree, None, "2", d, k, self.slot(tree, 0, d))
        self.sib(s, tree)

    def sib(self, s, tree):
        if self.bs is not None:
            self.to_sibling(s, s + 1 - 2 * self.c, tree)

    def steps(self):
        out = []
        def s0():
            for t in self.order:
                for d in (1, -1):
                    self.send(self.me, t, None, "1", d, 0, self.slot(t, d, 0))
            for t in self.order:
                self.fan(t, 0)
        out.append(s0)
        def s1():
            for d in (1, -1):
                for t in self.order:
                    s = self.slot(t, -d, 0)
                    self.wait(s, t, None, "1", d)
                    self.send(s, t, 0 if d > 0 else 1, "1q", d, 0, self.slot(t, d, 0))
            for t in self.order:
                for k in (1, 2):
                    self.fan(t, k)
        out.append(s1)
        def s2():
            for t in self.order:
                s = self.slot(t, 2, 0)
                self.wait(s, t, 0, "1q", 1)
                self.wait(s, t, 1, "1q", -1)
                self.fan(t, 3)
        out.append(s2)
        def s3(k):
            def f():
                for d in (1, -1):
                    for t in self.order:
                        s = self.slot(t, self.FIRST[k], -d)
                        self.wait(s, t, None, "2", d, k)
                        self.send(s, t, 0 if d > 0 else 1, "2q", d, k, self.slot(t, 0, d))
                        self.sib(s, t)
            return f
        def s4(k):
            def f():
                for t in self.order:
                    s = self.slot(t, self.FIRST[k], 2)
                    self.wait(s, t, 0, "2q", 1, k)
                    self.wait(s, t, 1, "2q", -1, k)
                    self.sib(s, t)
            return f
        out.insert(2, s3(0))
        out += [s3(1), s4(0), s3(2), s4(1), s3(3), s4(2), s4(3)]
        return out

    def wait_siblings(self):
        for _, r in self.sibs:
            r.wait_recv()

    def finish(self):
        for cp in self.sends:
            cp.wait_send()
        for cp, _ in self.sibs:
            cp.wait_send()


def place_of(me):
    chip = me // 2
    return lax.rem(chip, 4), chip // 4, lax.rem(me, 2)


def index_of(x, y, core):
    return (lax.rem(y + 4, 4) * 4 + lax.rem(x + 4, 4)) * 2 + core


def entry_barrier(me, after, before):
    x, y, core = place_of(me)
    barrier = pltpu.get_barrier_semaphore()
    near = [
        {"dp": index_of(x + 1, y, core)},
        {"dp": index_of(x - 1, y, core)},
        {"dp": index_of(x, y + 1, core)},
        {"dp": index_of(x, y - 1, core)},
        {"dp": me + 1 - 2 * core},
        {"section": after},
        {"section": before},
    ]
    for device in near:
        pl.semaphore_signal(barrier, inc=1, device_id=device, device_id_type=MESH)
    pl.semaphore_wait(barrier, len(near))


def contract_last(left, right):
    return lax.dot_general(
        left, right, (((1,), (1,)), ((), ())), preferred_element_type=jnp.float32
    )


def relay_kernel(
    lengths,
    held_hbm,
    norm_gain,
    w_in_hbm,
    q_gain,
    k_gain,
    w_out_hbm,
    out,
    held,
    normed,
    w_in,
    w_out,
    kv_sent,
    kv,
    q_sent,
    q,
    start_sent,
    start,
    cosine,
    sine,
    residual,
    keys,
    values,
    attended,
    local_sems,
    hop_send,
    hop_recv,
    in_send,
    in_recv,
    in_out_pair,
    in_in_pair,
    kv_send,
    kv_recv,
    kv_out_pair,
    kv_in_pair,
    out_send,
    out_recv,
    out_out_pair,
    out_in_pair,
):
    me = lax.axis_index("dp")
    section = lax.axis_index("section")
    after = lax.rem(section + 1, 8)
    before = lax.rem(section + 7, 8)
    columns_in = w_in.shape[0] // SLOTS
    columns_out = w_out.shape[0] // SLOTS

    def own_rows(ref, count):
        return ref.at[pl.ds(pl.multiple_of(me * count, 16), count), :]

    held_copy = pltpu.make_async_copy(held_hbm, held, local_sems.at[0])
    held_copy.start()
    own_copy = pltpu.make_async_copy(w_in_hbm, own_rows(w_in, columns_in), local_sems.at[1])
    own_copy.start()
    entry_barrier(me, after, before)

    def hop(source, target, number):
        return pltpu.make_async_remote_copy(
            source,
            target,
            hop_send.at[number],
            hop_recv.at[number],
            device_id={"section": after},
            device_id_type=MESH,
        )

    hop_w_out = hop(w_out_hbm, own_rows(w_out, columns_out), 0)
    hop_held = hop(held_hbm, residual, 1)
    hop_start = hop(start_sent, start, 2)
    hop_kv = hop(kv_sent, kv.at[me], 3)
    hop_q = [hop(q_sent.at[h], q.at[h], 4 + h) for h in range(KV_HEADS)]
    hop_w_out.start()
    hop_held.start()

    def by_columns(ref, count):
        def piece(slot, tree, quarter):
            rows = pl.ds(pl.multiple_of(slot * count, 16), count)
            base = 0 if tree == "A" else WIDTH // 2
            if quarter is None:
                return ref.at[rows, pl.ds(base, WIDTH // 2)]
            return ref.at[rows, pl.ds(base + WIDTH // 4 * quarter, WIDTH // 4)]

        return piece

    def by_rows(slot, tree, quarter):
        base = 0 if tree == "A" else ROWS
        if quarter is None:
            return kv.at[slot, pl.ds(base, ROWS), :]
        return kv.at[slot, pl.ds(base + ROWS // 2 * quarter, ROWS // 2), :]

    gather_in = Gather(by_columns(w_in, columns_in), in_send, in_recv, in_out_pair, in_in_pair)
    gather_kv = Gather(by_rows, kv_send, kv_recv, kv_out_pair, kv_in_pair)
    gather_out = Gather(
        by_columns(w_out, columns_out), out_send, out_recv, out_out_pair, out_in_pair
    )
    steps_in, steps_kv, steps_out = gather_in.steps(), gather_kv.steps(), gather_out.steps()

    own_copy.wait()
    steps_in[0]()

    lane = lax.broadcasted_iota(jnp.int32, (ROWS, HEAD), 1)
    token = me * ROWS + lax.broadcasted_iota(jnp.int32, (ROWS, HEAD), 0)
    low = lane < HEAD // 2
    pair = jnp.where(low, lane, lane - HEAD // 2).astype(jnp.float32)
    spacing = jnp.exp(pair * (-2.0 * math.log(THETA) / HEAD))
    for m in range(MICRO):
        end = lengths[m, 0]
        first = jnp.where(end <= token, end, 0)
        for j in range(1, 8):
            end = end + lengths[m, j]
            first = jnp.where(end <= token, end, first)
        rows = pl.ds(m * ROWS, ROWS)
        start_sent[rows, :] = first
        angle = (token - first).astype(jnp.float32) * spacing
        cosine[rows, :] = jnp.cos(angle)
        turn = jnp.sin(angle)
        sine[rows, :] = jnp.where(low, -turn, turn)
    hop_start.start()

    held_copy.wait()

    def norm_rows(i, carry):
        rows = pl.ds(pl.multiple_of(i * 32, 32), 32)
        x = held[rows, :].astype(jnp.float32)
        scale = lax.rsqrt(jnp.mean(x * x, axis=-1, keepdims=True) + EPSILON)
        normed[rows, :] = (x * scale * norm_gain[...]).astype(jnp.bfloat16)
        return carry

    for number in range(1, len(steps_in)):
        if number < 5:
            lax.fori_loop(2 * (number - 1), 2 * number, norm_rows, 0)
        steps_in[number]()

    def fill_ones(i, carry):
        rows = pl.ds(pl.multiple_of(i * ROWS, ROWS), ROWS)
        values[rows, pl.ds(HEAD, HEAD)] = jnp.ones((ROWS, HEAD), jnp.bfloat16)
        return carry

    lax.fori_loop(0, WINDOW, fill_ones, 0)
    hop_w_out.wait_recv()
    steps_out[0]()
    gather_in.wait_siblings()

    def turned(u, gain):
        scale = lax.rsqrt(jnp.mean(u * u, axis=-1, keepdims=True) + EPSILON)
        u = u * scale * gain
        return (u * cosine[...] + pltpu.roll(u, HEAD // 2, 1) * sine[...]).astype(jnp.bfloat16)

    def project(first):
        rows = pl.ds(pl.multiple_of(first, 2 * HEAD), 2 * HEAD)
        return contract_last(normed[...], w_in[rows, :])

    def as_slot(h, part):
        return pl.ds((h + 2 * part) * HEAD, HEAD)

    inner = HEADS * HEAD
    found = project(inner)
    for h in range(KV_HEADS):
        kv_sent[:, as_slot(h, 0)] = turned(found[:, h * HEAD : (h + 1) * HEAD], k_gain[...])
    found = project(inner + KV_HEADS * HEAD)
    for h in range(KV_HEADS):
        kv_sent[:, as_slot(h, 1)] = found[:, h * HEAD : (h + 1) * HEAD].astype(jnp.bfloat16)
    hop_kv.start()

    def query_pair(i, h):
        found = project((h * 4 + i) * 2 * HEAD)
        for k in range(2):
            u = turned(found[:, k * HEAD : (k + 1) * HEAD], q_gain[...])
            rows = pl.ds(pl.multiple_of((2 * i + k) * ROWS, ROWS), ROWS)
            for m in range(MICRO):
                q_sent[h, m, rows, :] = u[m * ROWS : (m + 1) * ROWS]
        return h

    lax.fori_loop(0, 2, lambda i, c: (query_pair(i, 0), c)[1], 0)
    hop_kv.wait_recv()
    steps_kv[0]()
    lax.fori_loop(2, 4, lambda i, c: (query_pair(i, 0), c)[1], 0)
    hop_q[0].start()
    steps_kv[1]()
    lax.fori_loop(0, 2, lambda i, c: (query_pair(i, 1), c)[1], 0)
    steps_kv[2]()
    lax.fori_loop(2, 4, lambda i, c: (query_pair(i, 1), c)[1], 0)
    hop_q[1].start()
    for step in steps_kv[3:]:
        step()
    gather_kv.wait_siblings()
    hop_start.wait_recv()

    scaled = math.log2(math.e) / math.sqrt(HEAD)
    own_row = lax.broadcasted_iota(jnp.int32, (ROWS, HEAD), 0)
    past = jnp.where(lane <= own_row, lane, -(1 << 20))

    def window(h, m):
        def one(j, carry):
            slot = lax.rem(me + SLOTS - (WINDOW - 1) + j, SLOTS)
            rows = pl.ds(pl.multiple_of(j * ROWS, ROWS), ROWS)
            here = pl.ds(m * ROWS, ROWS)
            keys[rows, :] = kv[slot, here, as_slot(h, 0)]
            values[rows, pl.ds(0, HEAD)] = kv[slot, here, as_slot(h, 1)]
            return carry

        lax.fori_loop(0, WINDOW, one, 0)

    def attend(h, m, i):
        rows = pl.ds(pl.multiple_of(i * 2 * ROWS, 2 * ROWS), 2 * ROWS)
        score = contract_last(q[h, m, rows, :], keys[...])
        since = start[pl.ds(m * ROWS, ROWS), :] - (me - (WINDOW - 1)) * ROWS
        for k in range(2):
            blocks = []
            for j in range(WINDOW):
                u = past if j == WINDOW - 1 else lane
                part = score[k * ROWS : (k + 1) * ROWS, j * HEAD : (j + 1) * HEAD]
                blocks.append(jnp.where(u + j * HEAD >= since, part, NEGATIVE))
            top = blocks[0]
            for part in blocks[1:]:
                top = jnp.maximum(top, part)
            top = jnp.max(top, axis=-1, keepdims=True) * scaled
            weight = jnp.concatenate(
                [jnp.exp2(part * scaled - top).astype(jnp.bfloat16) for part in blocks], axis=1
            )
            summed = jnp.dot(weight, values[...], preferred_element_type=jnp.float32)
            ratio = summed[:, :HEAD] / summed[:, HEAD:]
            columns = pl.ds(pl.multiple_of((h * GROUP + 2 * i + k) * HEAD, HEAD), HEAD)
            attended[pl.ds(m * ROWS, ROWS), columns] = ratio.astype(jnp.bfloat16)

    waiting = list(steps_out[1:])
    for h in range(KV_HEADS):
        hop_q[h].wait_recv()
        for m in range(MICRO):
            window(h, m)
            for half in range(2):
                lax.fori_loop(
                    2 * half, 2 * half + 2, lambda i, c: (attend(h, m, i), c)[1], 0
                )
                for _ in range(2):
                    if waiting:
                        waiting.pop(0)()
    for step in waiting:
        step()
    gather_out.wait_siblings()
    hop_held.wait_recv()

    def output(i, carry):
        columns = pl.ds(pl.multiple_of(i * 256, 256), 256)
        mixed = contract_last(attended[...], w_out[columns, :])
        out[:, columns] = (residual[:, columns].astype(jnp.float32) + mixed).astype(jnp.bfloat16)
        return carry

    lax.fori_loop(0, WIDTH // 256, output, 0)

    for gather in (gather_in, gather_kv, gather_out):
        gather.finish()
    for one in (hop_w_out, hop_held, hop_start, hop_kv, *hop_q):
        one.wait_send()


def on_device(held, norm_gain, w_qkv, q_gain, k_gain, w_out, lengths):
    micro, rows, width = held.shape[1:]
    bf16, f32, i32 = jnp.bfloat16, jnp.float32, jnp.int32
    tokens = micro * rows
    key_width = KV_HEADS * HEAD
    hbm = pl.BlockSpec(memory_space=pl.ANY)
    vmem = pl.BlockSpec(memory_space=pltpu.VMEM)
    sems = []
    for _ in range(3):
        sems += [pltpu.SemaphoreType.DMA((n,)) for n in (40, 40, 32, 32)]
    result = pl.pallas_call(
        relay_kernel,
        out_shape=jax.ShapeDtypeStruct((tokens, width), bf16),
        in_specs=[
            pl.BlockSpec(memory_space=pltpu.SMEM), hbm, vmem, hbm, vmem, vmem, hbm,
        ],
        out_specs=vmem,
        scratch_shapes=[
            pltpu.VMEM((tokens, width), bf16),
            pltpu.VMEM((tokens, width), bf16),
            pltpu.VMEM((w_qkv.shape[2] * SLOTS, width), bf16),
            pltpu.VMEM((w_out.shape[2] * SLOTS, width), bf16),
            pltpu.VMEM((tokens, 2 * key_width), bf16),
            pltpu.VMEM((SLOTS, tokens, 2 * key_width), bf16),
            pltpu.VMEM((KV_HEADS, micro, GROUP * rows, HEAD), bf16),
            pltpu.VMEM((KV_HEADS, micro, GROUP * rows, HEAD), bf16),
            pltpu.VMEM((tokens, HEAD), i32),
            pltpu.VMEM((tokens, HEAD), i32),
            pltpu.VMEM((tokens, HEAD), f32),
            pltpu.VMEM((tokens, HEAD), f32),
            pltpu.VMEM((tokens, width), bf16),
            pltpu.VMEM((WINDOW * rows, HEAD), bf16),
            pltpu.VMEM((WINDOW * rows, 2 * HEAD), bf16),
            pltpu.VMEM((tokens, width), bf16),
            pltpu.SemaphoreType.DMA((2,)),
            pltpu.SemaphoreType.DMA((6,)),
            pltpu.SemaphoreType.DMA((6,)),
            *sems,
        ],
        compiler_params=pltpu.CompilerParams(
            collective_id=0, has_side_effects=True, vmem_limit_bytes=56 << 20
        ),
        name="relay",
    )(
        lengths[0],
        held[0].reshape(tokens, width),
        norm_gain,
        w_qkv[0].T,
        q_gain,
        k_gain,
        w_out[0].T,
    )
    return result.reshape(1, micro, rows, width)


def solution(mesh):
    in_specs = (
        P("section", None, "dp", None),
        P("section", None),
        P("section", None, "dp"),
        P("section", None),
        P("section", None),
        P("section", None, "dp"),
        P("section", None, None),
    )
    out_specs = P("section", None, "dp", None)
    return jax.shard_map(
        on_device, mesh=mesh, in_specs=in_specs, out_specs=out_specs, check_vma=False
    )
```

```python
import math

import jax
import jax.numpy as jnp
from jax import lax
from jax.experimental import pallas as pl
from jax.experimental.pallas import tpu as pltpu
from jax.sharding import PartitionSpec as P

HEADS = 16
KV_HEADS = 2
HEAD = 128
GROUP = 8
MICRO = 2
ROWS = 128
WIDTH = 2048
SLOTS = 32
WINDOW = 17
EPSILON = 1e-06
THETA = 1000000.0
NEGATIVE = -1e30
MESH = pl.DeviceIdType.MESH


class Gather:
    def __init__(self, piece, send_sems, recv_sems, sib_send, sib_recv, own_src=None, order=("A","B")):
        self.piece = piece
        self.ss, self.rs, self.bs, self.br = send_sems, recv_sems, sib_send, sib_recv
        me = lax.axis_index("dp")
        self.me = me
        self.c = lax.rem(me, 2)
        chip = me // 2
        self.x = lax.rem(chip, 4)
        self.y = chip // 4
        self.order = order
        self.sends = []
        self.sib_n = 0
        self.sibs = []

    def dev(self, ox, oy):
        return (lax.rem(self.y + 4 + oy, 4) * 4 + lax.rem(self.x + 4 + ox, 4)) * 2 + self.c

    def off(self, tree, first, second):
        return (first, second) if tree == "A" else (second, first)

    def role(self, tree, kind, d, k=0):
        base = 0 if tree == "A" else 20
        di = 0 if d > 0 else 1
        return base + {"1": 0, "1q": 2, "2": 4, "2q": 12}[kind] + di + 2 * k

    def copy(self, slot, tree, quarter, role, target):
        ref = self.piece(slot, tree, quarter)
        cp = pltpu.make_async_remote_copy(ref, ref, self.ss.at[role], self.rs.at[role],
            device_id={"dp": target}, device_id_type=pl.DeviceIdType.MESH)
        return cp

    def send(self, slot, tree, quarter, kind, d, k, target):
        cp = self.copy(slot, tree, quarter, self.role(tree, kind, d, k), target)
        cp.start()
        self.sends.append(cp)

    def wait(self, slot, tree, quarter, kind, d, k=0):
        self.copy(slot, tree, quarter, self.role(tree, kind, d, k), self.me).wait_recv()

    def sib_copy(self, slot, tree, n):
        ref = self.piece(slot, tree, None)
        return pltpu.make_async_remote_copy(ref, ref, self.bs.at[n], self.br.at[n],
            device_id={"dp": self.me + 1 - 2 * self.c}, device_id_type=pl.DeviceIdType.MESH)

    def to_sibling(self, slot, other, tree):
        n = self.sib_n
        self.sib_n += 1
        cp = self.sib_copy(slot, tree, n)
        cp.start()
        self.sibs.append((cp, self.sib_copy(other, tree, n)))

    FIRST = (0, -1, 1, 2)

    def slot(self, tree, first, second):
        return self.dev(*self.off(tree, first, second))

    def fan(self, tree, k, part=None):
        s = self.slot(tree, self.FIRST[k], 0)
        for d in (1, -1):
            self.send(s, tree, None, "2", d, k, self.slot(tree, 0, d))
        self.sib(s, tree)

    def sib(self, s, tree):
        if self.bs is not None:
            self.to_sibling(s, s + 1 - 2 * self.c, tree)

    def steps(self):
        out = []
        def s0():
            for t in self.order:
                for d in (1, -1):
                    self.send(self.me, t, None, "1", d, 0, self.slot(t, d, 0))
            for t in self.order:
                self.fan(t, 0)
        out.append(s0)
        def s1():
            for d in (1, -1):
                for t in self.order:
                    s = self.slot(t, -d, 0)
                    self.wait(s, t, None, "1", d)
                    self.send(s, t, 0 if d > 0 else 1, "1q", d, 0, self.slot(t, d, 0))
            for t in self.order:
                for k in (1, 2):
                    self.fan(t, k)
        out.append(s1)
        def s2():
            for t in self.order:
                s = self.slot(t, 2, 0)
                self.wait(s, t, 0, "1q", 1)
                self.wait(s, t, 1, "1q", -1)
                self.fan(t, 3)
        out.append(s2)
        def s3(k):
            def f():
                for d in (1, -1):
                    for t in self.order:
                        s = self.slot(t, self.FIRST[k], -d)
                        self.wait(s, t, None, "2", d, k)
                        self.send(s, t, 0 if d > 0 else 1, "2q", d, k, self.slot(t, 0, d))
                        self.sib(s, t)
            return f
        def s4(k):
            def f():
                for t in self.order:
                    s = self.slot(t, self.FIRST[k], 2)
                    self.wait(s, t, 0, "2q", 1, k)
                    self.wait(s, t, 1, "2q", -1, k)
                    self.sib(s, t)
            return f
        out.insert(2, s3(0))
        out += [s3(1), s4(0), s3(2), s4(1), s3(3), s4(2), s4(3)]
        return out

    def wait_siblings(self):
        for _, r in self.sibs:
            r.wait_recv()

    def finish(self):
        for cp in self.sends:
            cp.wait_send()
        for cp, _ in self.sibs:
            cp.wait_send()


def place_of(me):
    chip = me // 2
    return lax.rem(chip, 4), chip // 4, lax.rem(me, 2)


def index_of(x, y, core):
    return (lax.rem(y + 4, 4) * 4 + lax.rem(x + 4, 4)) * 2 + core


def entry_barrier(me, after, before):
    x, y, core = place_of(me)
    barrier = pltpu.get_barrier_semaphore()
    near = [
        {"dp": index_of(x + 1, y, core)},
        {"dp": index_of(x - 1, y, core)},
        {"dp": index_of(x, y + 1, core)},
        {"dp": index_of(x, y - 1, core)},
        {"dp": me + 1 - 2 * core},
        {"section": after},
        {"section": before},
    ]
    for device in near:
        pl.semaphore_signal(barrier, inc=1, device_id=device, device_id_type=MESH)
    pl.semaphore_wait(barrier, len(near))


def contract_last(left, right):
    return lax.dot_general(
        left, right, (((1,), (1,)), ((), ())), preferred_element_type=jnp.float32
    )


def relay_kernel(
    lengths,
    held_hbm,
    norm_gain,
    w_in_hbm,
    q_gain,
    k_gain,
    w_out_hbm,
    out,
    held,
    normed,
    w_in,
    w_out,
    kv_sent,
    kv,
    q_sent,
    q,
    start_sent,
    start,
    cosine,
    sine,
    residual,
    keys,
    values,
    attended,
    local_sems,
    hop_send,
    hop_recv,
    in_send,
    in_recv,
    in_out_pair,
    in_in_pair,
    kv_send,
    kv_recv,
    kv_out_pair,
    kv_in_pair,
    out_send,
    out_recv,
    out_out_pair,
    out_in_pair,
):
    me = lax.axis_index("dp")
    section = lax.axis_index("section")
    after = lax.rem(section + 1, 8)
    before = lax.rem(section + 7, 8)
    columns_in = w_in.shape[0] // SLOTS
    columns_out = w_out.shape[0] // SLOTS

    def own_rows(ref, count):
        return ref.at[pl.ds(pl.multiple_of(me * count, 16), count), :]

    held_copy = pltpu.make_async_copy(held_hbm, held, local_sems.at[0])
    held_copy.start()
    own_copy = pltpu.make_async_copy(w_in_hbm, own_rows(w_in, columns_in), local_sems.at[1])
    own_copy.start()
    entry_barrier(me, after, before)

    def hop(source, target, number):
        return pltpu.make_async_remote_copy(
            source,
            target,
            hop_send.at[number],
            hop_recv.at[number],
            device_id={"section": after},
            device_id_type=MESH,
        )

    hop_w_out = hop(w_out_hbm, own_rows(w_out, columns_out), 0)
    hop_held = hop(held_hbm, residual, 1)
    hop_start = hop(start_sent, start, 2)
    hop_kv = hop(kv_sent, kv.at[me], 3)
    hop_q = [hop(q_sent.at[h], q.at[h], 4 + h) for h in range(KV_HEADS)]
    hop_w_out.start()
    hop_held.start()

    def by_columns(ref, count):
        def piece(slot, tree, quarter):
            rows = pl.ds(pl.multiple_of(slot * count, 16), count)
            base = 0 if tree == "A" else WIDTH // 2
            if quarter is None:
                return ref.at[rows, pl.ds(base, WIDTH // 2)]
            return ref.at[rows, pl.ds(base + WIDTH // 4 * quarter, WIDTH // 4)]

        return piece

    def by_rows(slot, tree, quarter):
        base = 0 if tree == "A" else ROWS
        if quarter is None:
            return kv.at[slot, pl.ds(base, ROWS), :]
        return kv.at[slot, pl.ds(base + ROWS // 2 * quarter, ROWS // 2), :]

    gather_in = Gather(by_columns(w_in, columns_in), in_send, in_recv, in_out_pair, in_in_pair)
    gather_kv = Gather(by_rows, kv_send, kv_recv, kv_out_pair, kv_in_pair)
    gather_out = Gather(
        by_columns(w_out, columns_out), out_send, out_recv, out_out_pair, out_in_pair
    )
    steps_in, steps_kv, steps_out = gather_in.steps(), gather_kv.steps(), gather_out.steps()

    own_copy.wait()
    steps_in[0]()

    lane = lax.broadcasted_iota(jnp.int32, (ROWS, HEAD), 1)
    token = me * ROWS + lax.broadcasted_iota(jnp.int32, (ROWS, HEAD), 0)
    low = lane < HEAD // 2
    pair = jnp.where(low, lane, lane - HEAD // 2).astype(jnp.float32)
    spacing = jnp.exp(pair * (-2.0 * math.log(THETA) / HEAD))
    for m in range(MICRO):
        end = lengths[m, 0]
        first = jnp.where(end <= token, end, 0)
        for j in range(1, 8):
            end = end + lengths[m, j]
            first = jnp.where(end <= token, end, first)
        rows = pl.ds(m * ROWS, ROWS)
        start_sent[rows, :] = first
        angle = (token - first).astype(jnp.float32) * spacing
        cosine[rows, :] = jnp.cos(angle)
        turn = jnp.sin(angle)
        sine[rows, :] = jnp.where(low, -turn, turn)
    hop_start.start()

    held_copy.wait()

    def norm_rows(i, carry):
        rows = pl.ds(pl.multiple_of(i * 32, 32), 32)
        x = held[rows, :].astype(jnp.float32)
        scale = lax.rsqrt(jnp.mean(x * x, axis=-1, keepdims=True) + EPSILON)
        normed[rows, :] = (x * scale * norm_gain[...]).astype(jnp.bfloat16)
        return carry

    for number in range(1, len(steps_in)):
        if number < 5:
            lax.fori_loop(2 * (number - 1), 2 * number, norm_rows, 0)
        steps_in[number]()

    def fill_ones(i, carry):
        rows = pl.ds(pl.multiple_of(i * ROWS, ROWS), ROWS)
        values[rows, pl.ds(HEAD, HEAD)] = jnp.ones((ROWS, HEAD), jnp.bfloat16)
        return carry

    lax.fori_loop(0, WINDOW, fill_ones, 0)
    hop_w_out.wait_recv()
    steps_out[0]()
    gather_in.wait_siblings()

    def turned(u, gain):
        scale = lax.rsqrt(jnp.mean(u * u, axis=-1, keepdims=True) + EPSILON)
        u = u * scale * gain
        return (u * cosine[...] + pltpu.roll(u, HEAD // 2, 1) * sine[...]).astype(jnp.bfloat16)

    def project(first):
        rows = pl.ds(pl.multiple_of(first, 2 * HEAD), 2 * HEAD)
        return contract_last(normed[...], w_in[rows, :])

    def as_slot(h, part):
        return pl.ds((h + 2 * part) * HEAD, HEAD)

    inner = HEADS * HEAD
    found = project(inner)
    for h in range(KV_HEADS):
        kv_sent[:, as_slot(h, 0)] = turned(found[:, h * HEAD : (h + 1) * HEAD], k_gain[...])
    found = project(inner + KV_HEADS * HEAD)
    for h in range(KV_HEADS):
        kv_sent[:, as_slot(h, 1)] = found[:, h * HEAD : (h + 1) * HEAD].astype(jnp.bfloat16)
    hop_kv.start()

    def query_pair(i, h):
        found = project((h * 4 + i) * 2 * HEAD)
        for k in range(2):
            u = turned(found[:, k * HEAD : (k + 1) * HEAD], q_gain[...])
            rows = pl.ds(pl.multiple_of((2 * i + k) * ROWS, ROWS), ROWS)
            for m in range(MICRO):
                q_sent[h, m, rows, :] = u[m * ROWS : (m + 1) * ROWS]
        return h

    lax.fori_loop(0, 2, lambda i, c: (query_pair(i, 0), c)[1], 0)
    hop_kv.wait_recv()
    steps_kv[0]()
    lax.fori_loop(2, 4, lambda i, c: (query_pair(i, 0), c)[1], 0)
    hop_q[0].start()
    steps_kv[1]()
    lax.fori_loop(0, 2, lambda i, c: (query_pair(i, 1), c)[1], 0)
    steps_kv[2]()
    lax.fori_loop(2, 4, lambda i, c: (query_pair(i, 1), c)[1], 0)
    hop_q[1].start()
    steps_kv[3]()
    steps_kv[4]()
    steps_kv[5]()
    steps_kv[6]()
    steps_kv[7]()
    steps_kv[8]()
    steps_out[1]()
    steps_kv[9]()
    steps_out[2]()
    steps_kv[10]()
    gather_kv.wait_siblings()
    hop_start.wait_recv()

    scaled = math.log2(math.e) / math.sqrt(HEAD)
    own_row = lax.broadcasted_iota(jnp.int32, (ROWS, HEAD), 0)
    past = jnp.where(lane <= own_row, lane, -(1 << 20))

    def window(h, m):
        def one(j, carry):
            slot = lax.rem(me + SLOTS - (WINDOW - 1) + j, SLOTS)
            rows = pl.ds(pl.multiple_of(j * ROWS, ROWS), ROWS)
            here = pl.ds(m * ROWS, ROWS)
            keys[rows, :] = kv[slot, here, as_slot(h, 0)]
            values[rows, pl.ds(0, HEAD)] = kv[slot, here, as_slot(h, 1)]
            return carry

        lax.fori_loop(0, WINDOW, one, 0)

    def attend(h, m, i):
        rows = pl.ds(pl.multiple_of(i * 2 * ROWS, 2 * ROWS), 2 * ROWS)
        score = contract_last(q[h, m, rows, :], keys[...])
        since = start[pl.ds(m * ROWS, ROWS), :] - (me - (WINDOW - 1)) * ROWS
        for k in range(2):
            blocks = []
            for j in range(WINDOW):
                u = past if j == WINDOW - 1 else lane
                part = score[k * ROWS : (k + 1) * ROWS, j * HEAD : (j + 1) * HEAD]
                blocks.append(jnp.where(u + j * HEAD >= since, part, NEGATIVE))
            top = blocks[0]
            for part in blocks[1:]:
                top = jnp.maximum(top, part)
            top = jnp.max(top, axis=-1, keepdims=True) * scaled
            weight = jnp.concatenate(
                [jnp.exp2(part * scaled - top).astype(jnp.bfloat16) for part in blocks], axis=1
            )
            summed = jnp.dot(weight, values[...], preferred_element_type=jnp.float32)
            ratio = summed[:, :HEAD] / summed[:, HEAD:]
            columns = pl.ds(pl.multiple_of((h * GROUP + 2 * i + k) * HEAD, HEAD), HEAD)
            attended[pl.ds(m * ROWS, ROWS), columns] = ratio.astype(jnp.bfloat16)

    between = [[3], [4], [5], [6], [7], [8], [9], [10]]
    for h in range(KV_HEADS):
        hop_q[h].wait_recv()
        for m in range(MICRO):
            window(h, m)
            for half in range(2):
                lax.fori_loop(
                    2 * half, 2 * half + 2, lambda i, c: (attend(h, m, i), c)[1], 0
                )
                for number in between[h * 4 + m * 2 + half]:
                    steps_out[number]()
    for number in []:
        steps_out[number]()
    gather_out.wait_siblings()
    hop_held.wait_recv()

    def output(i, carry):
        columns = pl.ds(pl.multiple_of(i * 256, 256), 256)
        mixed = contract_last(attended[...], w_out[columns, :])
        out[:, columns] = (residual[:, columns].astype(jnp.float32) + mixed).astype(jnp.bfloat16)
        return carry

    lax.fori_loop(0, WIDTH // 256, output, 0)

    for gather in (gather_in, gather_kv, gather_out):
        gather.finish()
    for one in (hop_w_out, hop_held, hop_start, hop_kv, *hop_q):
        one.wait_send()


def on_device(held, norm_gain, w_qkv, q_gain, k_gain, w_out, lengths):
    micro, rows, width = held.shape[1:]
    bf16, f32, i32 = jnp.bfloat16, jnp.float32, jnp.int32
    tokens = micro * rows
    key_width = KV_HEADS * HEAD
    hbm = pl.BlockSpec(memory_space=pl.ANY)
    vmem = pl.BlockSpec(memory_space=pltpu.VMEM)
    sems = []
    for _ in range(3):
        sems += [pltpu.SemaphoreType.DMA((n,)) for n in (40, 40, 32, 32)]
    result = pl.pallas_call(
        relay_kernel,
        out_shape=jax.ShapeDtypeStruct((tokens, width), bf16),
        in_specs=[
            pl.BlockSpec(memory_space=pltpu.SMEM), hbm, vmem, hbm, vmem, vmem, hbm,
        ],
        out_specs=vmem,
        scratch_shapes=[
            pltpu.VMEM((tokens, width), bf16),
            pltpu.VMEM((tokens, width), bf16),
            pltpu.VMEM((w_qkv.shape[2] * SLOTS, width), bf16),
            pltpu.VMEM((w_out.shape[2] * SLOTS, width), bf16),
            pltpu.VMEM((tokens, 2 * key_width), bf16),
            pltpu.VMEM((SLOTS, tokens, 2 * key_width), bf16),
            pltpu.VMEM((KV_HEADS, micro, GROUP * rows, HEAD), bf16),
            pltpu.VMEM((KV_HEADS, micro, GROUP * rows, HEAD), bf16),
            pltpu.VMEM((tokens, HEAD), i32),
            pltpu.VMEM((tokens, HEAD), i32),
            pltpu.VMEM((tokens, HEAD), f32),
            pltpu.VMEM((tokens, HEAD), f32),
            pltpu.VMEM((tokens, width), bf16),
            pltpu.VMEM((WINDOW * rows, HEAD), bf16),
            pltpu.VMEM((WINDOW * rows, 2 * HEAD), bf16),
            pltpu.VMEM((tokens, width), bf16),
            pltpu.SemaphoreType.DMA((2,)),
            pltpu.SemaphoreType.DMA((6,)),
            pltpu.SemaphoreType.DMA((6,)),
            *sems,
        ],
        compiler_params=pltpu.CompilerParams(
            collective_id=0, has_side_effects=True, vmem_limit_bytes=56 << 20
        ),
        name="relay",
    )(
        lengths[0],
        held[0].reshape(tokens, width),
        norm_gain,
        w_qkv[0].T,
        q_gain,
        k_gain,
        w_out[0].T,
    )
    return result.reshape(1, micro, rows, width)


def solution(mesh):
    in_specs = (
        P("section", None, "dp", None),
        P("section", None),
        P("section", None, "dp"),
        P("section", None),
        P("section", None),
        P("section", None, "dp"),
        P("section", None, None),
    )
    out_specs = P("section", None, "dp", None)
    return jax.shard_map(
        on_device, mesh=mesh, in_specs=in_specs, out_specs=out_specs, check_vma=False
    )
```
